512 devices in a mesh: tm: 4 (over z_hi, core), height: 16 (over x, y), panel: 8 (over z_lo).
Axes of the slice: x: 4, y: 4, z: 16 (z_hi: 2, z_lo: 8; z = z_hi * 8 + z_lo), core: 2. Of those that a mesh axis runs over, the one named last changes fastest.
Arguments:
- activations: bfloat16 [6, 8, 32, 512, 128], P(None, 'tm', 'height', 'panel'), may hold values from -6 to 6
- out_grad: bfloat16 [6, 8, 32, 512, 128], P(None, 'tm', 'height'), may hold values from -0.019042969 to 0.019042969
- out_basis: bfloat16 [512, 512], replicated, may hold values from -0.25 to 0.25
- in_basis: bfloat16 [13824, 13824], P('panel', ('tm', 'height')), may hold values from -0.0546875 to 0.0546875
- eigenvalues: float32 [512, 13824], P('panel', ('tm', 'height')), may hold values from 0.05 to 5
- forget_order: int32 [6], replicated, may hold values from 0 to 5, each once
Outputs:
- correction: float32 [512, 13824], P('panel', ('tm', 'height'))
The draws below stay inside these ranges and needn't reach their ends.
Inputs may be any that keep to these rules, and one draw needn't show every extreme that they name: `forget_order`: a permutation of the clip ids.
All inputs are finite; a program needn't handle non-finite values.
Results may differ from the reference program's by a relative error of at most 0.0041.
Values may be sent and summed in bfloat16 or wider, within the bound.
A program may use at most 64 MiB of HBM per device.

```python
import math
import jax
import jax.numpy as jnp

COUT = 512
CIN = 512
WID = 128
CLIPS = 6
FORGET = 3
FRAMES = 8
ROWS = 32
FEAT = 13824
POSITIONS = 98304


def levels(rng, extent, pieces, least, top_value):
    loudness = 1.0
    for axis_at, parts in pieces:
        heights = jax.random.uniform(jax.random.fold_in(jax.random.fold_in(rng, 6), axis_at), (parts,), jnp.float32, least / len(pieces), top_value / len(pieces))
        loudness = loudness * jnp.repeat(jnp.exp(heights), extent[axis_at] // parts).reshape((-1,) + (1,) * (len(extent) - 1 - axis_at))
    return loudness


def gaussian(own_key, shape, width, reach, shards=(), held_as=jnp.bfloat16):
    level = levels(own_key, shape, shards, -0.22, 0.18) if shards else 1.0
    entries = jax.random.normal(own_key, shape, jnp.float32) * width * level
    return jnp.minimum(jnp.maximum(entries, -reach), reach).astype(held_as)


def setup_inputs(seed: int = 0) -> dict:
    key_list = jax.random.split(jax.random.key(seed), 7)
    return {
        "activations": gaussian(key_list[0], (CLIPS, FRAMES, ROWS, CIN, WID), 1.0, 6.0, ((1, 4), (2, 16), (3, 8))),
        "out_grad": gaussian(key_list[1], (CLIPS, FRAMES, ROWS, COUT, WID), (1 / POSITIONS ** 0.5), 0.019042969, ((1, 4), (2, 16))),
        "out_basis": gaussian(key_list[2], (COUT, COUT), COUT ** -0.5, 0.25),
        "in_basis": gaussian(key_list[3], (FEAT, FEAT), FEAT ** -0.5, 0.0546875, ((0, 8), (1, 64))),
        "eigenvalues": jnp.clip(jnp.exp(math.log(5.0) - 4.6051702 * jax.random.uniform(key_list[4], (COUT, FEAT), jnp.float32) ** levels(key_list[4], (COUT, FEAT), ((0, 8), (1, 64)), -0.2, 0.2)), 0.05, 5.0),
        "forget_order": jax.random.permutation(key_list[5], CLIPS).astype(jnp.int32),
    }


def reference(activations, out_grad, out_basis, in_basis, eigenvalues, forget_order):
    chosen = forget_order[:FORGET].astype(jnp.int32)
    sel_act = jnp.take(activations, chosen, axis=0)
    sel_grad = jnp.take(out_grad, chosen, axis=0)
    projected = jnp.einsum('nfrow,ok->nfrkw', sel_grad.astype(jnp.float32), out_basis.astype(jnp.float32))
    projected = projected.astype(jnp.bfloat16).astype(jnp.float32)
    padded = jnp.pad(sel_act, ((0, 0), (2, 0), (1, 1), (0, 0), (1, 1))).astype(jnp.float32)
    frames = sel_act.shape[1]
    rows = sel_act.shape[2]
    wide = sel_act.shape[4]
    terms = []
    for shift_t in range(3):
        for shift_h in range(3):
            for shift_w in range(3):
                window = padded[:, shift_t:shift_t + frames, shift_h:shift_h + rows, :, shift_w:shift_w + wide]
                terms.append(jnp.einsum('nfrkw,nfrcw->kc', projected, window))
    grad = jnp.stack(terms, axis=2).reshape(COUT, CIN * 27).astype(jnp.bfloat16)
    rotated = jnp.dot(grad, in_basis, preferred_element_type=jnp.float32)
    return rotated / (eigenvalues + 0.1)
```

```python
import functools

import jax
import jax.numpy as jnp
import numpy as np
from jax import lax
from jax.experimental import pallas as pl
from jax.experimental.pallas import tpu as pltpu
from jax.sharding import PartitionSpec as P

FORGET = 3
TAPS = 27
LANES = 128
SUB = 8
CHIPS = 16
PANELS = 8
MESH = pl.DeviceIdType.MESH


damping = 0.1


def from_behind(value, axis, steps):
    count = lax.axis_size(axis)
    leading, last = (max(0, -steps), min(count, count - steps))
    return lax.ppermute(value, axis, [(source, source + steps) for source in range(leading, last)])


def with_halo(block, sides, width):
    for axis, dim in sides:
        count = lax.axis_size(axis)
        forward = [(i, i + 1) for i in range(count - 1)]
        backward = [(target, source) for source, target in forward]
        low = lax.ppermute(
            lax.slice_in_dim(block, block.shape[dim] - width, None, axis=dim), axis, forward
        )
        high = lax.ppermute(lax.slice_in_dim(block, 0, width, axis=dim), axis, backward)
        block = jnp.concatenate([low, block, high], axis=dim)
    return block


def sum_kernel(
    t_ref,
    g_ref,
    c_buf,
    s_buf,
    r_buf,
    acc,
    z_out,
    z_in,
    c_send,
    c_recv,
    s_send,
    s_recv,
    z_send,
    z_recv,
    g_send,
    g_recv,
    f_send,
    f_recv,
):
    tm = lax.axis_index("tm")
    me = lax.axis_index("height")
    core = lax.rem(tm, 2)
    mate = tm + 1 - 2 * core
    far = lax.rem(tm + 2, 4)
    rows = TAPS * SUB

    barrier = pltpu.get_barrier_semaphore()
    pl.semaphore_signal(barrier, inc=1, device_id={"tm": mate}, device_id_type=MESH)
    pl.semaphore_signal(barrier, inc=1, device_id={"tm": far}, device_id_type=MESH)

    @pl.loop(1, CHIPS)
    def _(d):
        pl.semaphore_signal(
            barrier, inc=1, device_id={"height": lax.rem(me + d, CHIPS)}, device_id_type=MESH
        )

    pl.semaphore_wait(barrier, CHIPS + 1)

    def c_rows(i):
        return pl.ds(pl.multiple_of(lax.rem(me + i, SUB) * SUB, SUB), SUB)

    def pair_copy(i):
        half = pl.ds(pl.multiple_of((1 - core) * 256, 256), 256)
        return pltpu.make_async_remote_copy(
            src_ref=t_ref.at[:, c_rows(i), half],
            dst_ref=c_buf.at[i],
            send_sem=c_send.at[i],
            recv_sem=c_recv.at[i],
            device_id={"tm": mate},
            device_id_type=MESH,
        )

    @pl.loop(0, SUB)
    def _(i):
        pair_copy(i).start()

    def plane_copy(d):
        return pltpu.make_async_remote_copy(
            src_ref=s_buf.at[d],
            dst_ref=r_buf.at[d],
            send_sem=s_send.at[d],
            recv_sem=s_recv.at[d],
            device_id={"height": lax.rem(me + d, CHIPS)},
            device_id_type=MESH,
        )

    def chunk(i, d):
        low = lax.rem(me + d, CHIPS) // SUB
        own = t_ref[
            :, c_rows(i), pl.ds(pl.multiple_of((2 * core + low) * LANES, LANES), LANES)
        ]
        other = c_buf[i, :, :, pl.ds(pl.multiple_of(low * LANES, LANES), LANES)]
        return (own + other).reshape(rows, LANES)

    pair_copy(0).wait_recv()
    s_buf[SUB] = chunk(0, SUB).astype(jnp.bfloat16)
    plane_copy(SUB).start()
    acc[...] = chunk(0, 0)

    @pl.loop(1, SUB)
    def _(i):
        pair_copy(i).wait_recv()
        s_buf[i] = chunk(i, i).astype(jnp.bfloat16)
        plane_copy(i).start()
        s_buf[i + SUB] = chunk(i, i + SUB).astype(jnp.bfloat16)
        plane_copy(i + SUB).start()

    @pl.loop(1, CHIPS)
    def _(d):
        plane_copy(d).wait_recv()
        acc[...] += r_buf[d].astype(jnp.float32)

    z_out[...] = acc[...].astype(jnp.bfloat16)
    z_copy = pltpu.make_async_remote_copy(
        src_ref=z_out,
        dst_ref=z_in,
        send_sem=z_send,
        recv_sem=z_recv,
        device_id={"tm": far},
        device_id_type=MESH,
    )
    z_copy.start()
    z_copy.wait_recv()

    def slot(d):
        owner = lax.rem(me - d + CHIPS, CHIPS)
        return (2 * core + owner // SUB) * SUB + lax.rem(owner, SUB)

    def gather_copy(d):
        return pltpu.make_async_remote_copy(
            src_ref=g_ref.at[slot(0)],
            dst_ref=g_ref.at[slot(0)],
            send_sem=g_send.at[d],
            recv_sem=g_recv.at[d],
            device_id={"height": lax.rem(me + d, CHIPS)},
            device_id_type=MESH,
        )

    def hand_copy(d):
        return pltpu.make_async_remote_copy(
            src_ref=g_ref.at[slot(d)],
            dst_ref=g_ref.at[slot(d)],
            send_sem=f_send.at[d],
            recv_sem=f_recv.at[d],
            device_id={"tm": mate},
            device_id_type=MESH,
        )

    g_ref[slot(0)] = (acc[...] + z_in[...].astype(jnp.float32)).astype(jnp.bfloat16)

    @pl.loop(1, CHIPS)
    def _(d):
        gather_copy(d).start()

    hand_copy(0).start()

    @pl.loop(1, CHIPS)
    def _(d):
        gather_copy(d).wait_recv()
        hand_copy(d).start()

    @pl.loop(0, SUB)
    def _(i):
        pair_copy(i).wait_send()

    z_copy.wait_send()
    hand_copy(0).wait()

    @pl.loop(1, CHIPS)
    def _(d):
        plane_copy(d).wait_send()
        gather_copy(d).wait_send()
        hand_copy(d).wait()


def sum_gradient(partial):
    rows = TAPS * SUB
    dma = pltpu.SemaphoreType.DMA
    return pl.pallas_call(
        sum_kernel,
        out_shape=jax.ShapeDtypeStruct((4 * SUB, rows, LANES), jnp.bfloat16),
        in_specs=[pl.BlockSpec(memory_space=pltpu.VMEM)],
        out_specs=pl.BlockSpec(memory_space=pltpu.VMEM),
        scratch_shapes=[
            pltpu.VMEM((SUB, TAPS, SUB, 2 * LANES), jnp.float32),
            pltpu.VMEM((CHIPS, rows, LANES), jnp.bfloat16),
            pltpu.VMEM((CHIPS, rows, LANES), jnp.bfloat16),
            pltpu.VMEM((rows, LANES), jnp.float32),
            pltpu.VMEM((rows, LANES), jnp.bfloat16),
            pltpu.VMEM((rows, LANES), jnp.bfloat16),
            dma((SUB,)),
            dma((SUB,)),
            dma((CHIPS,)),
            dma((CHIPS,)),
            dma(()),
            dma(()),
            dma((CHIPS,)),
            dma((CHIPS,)),
            dma((CHIPS,)),
            dma((CHIPS,)),
        ],
        compiler_params=pltpu.CompilerParams(collective_id=0, has_side_effects=True),
    )(partial)


def panel_kernel(rot_ref, eig_ref, out_ref, s_buf, r_buf, s_send, s_recv):
    me = lax.axis_index("panel")
    barrier = pltpu.get_barrier_semaphore()

    @pl.loop(1, PANELS)
    def _(d):
        pl.semaphore_signal(
            barrier, inc=1, device_id={"panel": lax.rem(me + d, PANELS)}, device_id_type=MESH
        )

    pl.semaphore_wait(barrier, PANELS - 1)

    def copy(d):
        return pltpu.make_async_remote_copy(
            src_ref=s_buf.at[d],
            dst_ref=r_buf.at[d],
            send_sem=s_send.at[d],
            recv_sem=s_recv.at[d],
            device_id={"panel": lax.rem(me + d, PANELS)},
            device_id_type=MESH,
        )

    @pl.loop(1, PANELS)
    def _(d):
        s_buf[d] = rot_ref[lax.rem(me + d, PANELS)].astype(jnp.bfloat16)
        copy(d).start()

    out_ref[...] = rot_ref[me]

    @pl.loop(1, PANELS)
    def _(d):
        copy(d).wait_recv()
        out_ref[...] += r_buf[d].astype(jnp.float32)

    out_ref[...] = out_ref[...] / (eig_ref[...] + damping)

    @pl.loop(1, PANELS)
    def _(d):
        copy(d).wait_send()


def finish(rotated, eigenvalues):
    _, height, width = rotated.shape
    vmem = pl.BlockSpec(memory_space=pltpu.VMEM)
    return pl.pallas_call(
        panel_kernel,
        out_shape=jax.ShapeDtypeStruct((height, width), jnp.float32),
        in_specs=[vmem, vmem],
        out_specs=vmem,
        scratch_shapes=[
            pltpu.VMEM((PANELS, height, width), jnp.bfloat16),
            pltpu.VMEM((PANELS, height, width), jnp.bfloat16),
            pltpu.SemaphoreType.DMA((PANELS,)),
            pltpu.SemaphoreType.DMA((PANELS,)),
        ],
        compiler_params=pltpu.CompilerParams(collective_id=1, has_side_effects=True),
    )(rotated, eigenvalues)


def tap_major(in_basis):
    block = TAPS * SUB
    source = np.arange(block).reshape(SUB, TAPS).T.reshape(-1)
    pick = jnp.asarray(np.eye(block, dtype=np.float32)[source], jnp.bfloat16)
    blocks = in_basis.reshape(-1, block, in_basis.shape[1])
    return jnp.einsum("sr,brj->bsj", pick, blocks, preferred_element_type=jnp.bfloat16)


def body(activations, out_grad, out_basis, in_basis, eigenvalues, forget_order):
    chosen = forget_order[:FORGET]
    sel_act = jnp.take(activations, chosen, axis=0)
    sel_grad = jnp.take(out_grad, chosen, axis=0)
    frames = sel_act.shape[1]
    rows = sel_act.shape[2]
    wide = sel_act.shape[4]
    projected = jnp.einsum(
        "nfrow,ok->nfrkw", sel_grad, out_basis, preferred_element_type=jnp.float32
    ).astype(jnp.bfloat16)
    previous = from_behind(sel_act, "tm", 1)
    extended = jnp.concatenate([previous, sel_act], axis=1)
    rimmed = with_halo(extended, (("height", 2),), 1)
    padded = jnp.pad(rimmed, ((0, 0), (0, 0), (0, 0), (0, 0), (1, 1)))
    windows = []
    for shift_t in range(3):
        for shift_h in range(3):
            for shift_w in range(3):
                windows.append(
                    padded[
                        :,
                        shift_t : shift_t + frames,
                        shift_h : shift_h + rows,
                        :,
                        shift_w : shift_w + wide,
                    ]
                )
    stacked = jnp.stack(windows, axis=0)
    partial_grad = jnp.einsum(
        "nfrkw,tnfrcw->tck", projected, stacked, preferred_element_type=jnp.float32
    )
    grad = sum_gradient(partial_grad)
    basis = tap_major(in_basis)
    grad = grad.reshape(4, in_basis.shape[0], LANES)
    basis = basis.reshape(in_basis.shape)
    rotated = jnp.einsum("ark,rj->akj", grad, basis, preferred_element_type=jnp.float32)
    rotated = rotated.reshape(PANELS, -1, in_basis.shape[1])
    return finish(rotated, eigenvalues)


def solution(mesh):
    in_specs = (
        P(None, "tm", "height", "panel", None),
        P(None, "tm", "height", None, None),
        P(),
        P("panel", ("tm", "height")),
        P("panel", ("tm", "height")),
        P(),
    )
    out_specs = P("panel", ("tm", "height"))
    return jax.shard_map(body, mesh=mesh, in_specs=in_specs, out_specs=out_specs, check_vma=False)
```

```python
import jax
import jax.numpy as jnp
from jax import lax
from jax.experimental import pallas as pl
from jax.experimental.pallas import tpu as pltpu
from jax.sharding import PartitionSpec as P

FORGET = 3
TAPS = 27
LANES = 128
SUB = 8
SLABS = 4
CHIPS = 16
PANELS = 8
BLOCKS = 12
CHANNELS = 64
OUT = 512
ROWS = TAPS * SUB
MESH = pl.DeviceIdType.MESH


damping = 0.1


def kernel(
    order_ref,
    act_ref,
    grad_ref,
    ob_ref,
    bt_ref,
    eig_ref,
    out_ref,
    e_buf,
    w_buf,
    p_buf,
    t_buf,
    c_buf,
    s_buf,
    r_buf,
    acc,
    z_out,
    z_in,
    g_buf,
    b_buf,
    rot_buf,
    fin_buf,
    q_buf,
    y_buf,
    h_send,
    h_recv,
    c_send,
    c_recv,
    s_send,
    s_recv,
    z_send,
    z_recv,
    g_send,
    g_recv,
    f_send,
    f_recv,
    q_send,
    q_recv,
):
    tm = lax.axis_index("tm")
    me = lax.axis_index("height")
    panel = lax.axis_index("panel")
    core = lax.rem(tm, 2)
    mate = tm + 1 - 2 * core
    far = lax.rem(tm + 2, SLABS)
    up = lax.rem(me + 1, CHIPS)
    down = lax.rem(me + CHIPS - 1, CHIPS)

    barrier = pltpu.get_barrier_semaphore()
    for axis, mine, count in (("tm", tm, SLABS), ("height", me, CHIPS), ("panel", panel, PANELS)):

        @pl.loop(1, count)
        def _(d):
            pl.semaphore_signal(
                barrier, inc=1, device_id={axis: lax.rem(mine + d, count)}, device_id_type=MESH
            )

    for n in range(FORGET):
        e_buf[n, 2:4, 1:3] = act_ref[order_ref[n]]

    @pl.when(tm == 0)
    def _():
        e_buf[:, 0:2] = jnp.zeros_like(e_buf[:, 0:2])

    @pl.when(me == 0)
    def _():
        e_buf[:, :, 0:1] = jnp.zeros_like(e_buf[:, :, 0:1])

    @pl.when(me == CHIPS - 1)
    def _():
        e_buf[:, :, 3:4] = jnp.zeros_like(e_buf[:, :, 3:4])

    def halo(i):
        source, target, device = (
            ((slice(2, 4), slice(1, 3)), (slice(0, 2), slice(1, 3)), {"tm": lax.rem(tm + 1, SLABS)}),
            ((slice(2, 4), slice(2, 3)), (slice(2, 4), slice(0, 1)), {"height": up}),
            ((slice(2, 4), slice(1, 2)), (slice(2, 4), slice(3, 4)), {"height": down}),
            ((slice(0, 2), slice(2, 3)), (slice(0, 2), slice(0, 1)), {"height": up}),
            ((slice(0, 2), slice(1, 2)), (slice(0, 2), slice(3, 4)), {"height": down}),
        )[i]
        return pltpu.make_async_remote_copy(
            src_ref=e_buf.at[(slice(None),) + source],
            dst_ref=e_buf.at[(slice(None),) + target],
            send_sem=h_send.at[i],
            recv_sem=h_recv.at[i],
            device_id=device,
            device_id_type=MESH,
        )

    sends = (
        tm < SLABS - 1,
        me < CHIPS - 1,
        me > 0,
        jnp.logical_and(tm > 0, me < CHIPS - 1),
        jnp.logical_and(tm > 0, me > 0),
    )
    receives = (
        tm > 0,
        me > 0,
        me < CHIPS - 1,
        jnp.logical_and(tm > 0, me > 0),
        jnp.logical_and(tm > 0, me < CHIPS - 1),
    )

    pl.semaphore_wait(barrier, SLABS + CHIPS + PANELS - 3)
    for i in range(3):

        @pl.when(sends[i])
        def _():
            halo(i).start()

    @pl.loop(0, BLOCKS)
    def _(b):
        block = grad_ref[order_ref[b // 4], lax.rem(b // 2, 2), lax.rem(b, 2)]
        rows = pl.ds(pl.multiple_of(b * LANES, LANES), LANES)
        p_buf[rows, :] = lax.dot_general(
            block, ob_ref[...], (((0,), (0,)), ((), ())), preferred_element_type=jnp.float32
        ).astype(jnp.bfloat16)

    def half(which):
        return pl.ds(pl.multiple_of(which * 2 * LANES, 2 * LANES), 2 * LANES)

    def pair_copy(dt):
        return pltpu.make_async_remote_copy(
            src_ref=t_buf.at[pl.ds(dt * 9, 9), :, half(1 - core)],
            dst_ref=c_buf.at[pl.ds(dt * 9, 9)],
            send_sem=c_send.at[dt],
            recv_sem=c_recv.at[dt],
            device_id={"tm": mate},
            device_id_type=MESH,
        )

    column = lax.broadcasted_iota(jnp.int32, (CHANNELS, LANES), 1)

    def taps_of(dt):
        @pl.loop(0, BLOCKS)
        def _(b):
            n, f, r = b // 4, lax.rem(b // 2, 2), lax.rem(b, 2)
            lanes = pl.ds(pl.multiple_of(b * LANES, LANES), LANES)
            for dh in range(3):
                tile = e_buf[n, f + dt, r + dh]
                wide = tile.astype(jnp.float32)
                left = jnp.where(column == 0, 0.0, pltpu.roll(wide, 1, 1)).astype(jnp.bfloat16)
                right = jnp.where(column == LANES - 1, 0.0, pltpu.roll(wide, LANES - 1, 1)).astype(
                    jnp.bfloat16
                )
                for dw, shifted in enumerate((left, tile, right)):
                    at = (dt * 9 + dh * 3 + dw) * CHANNELS
                    w_buf[at : at + CHANNELS, lanes] = shifted

        at = dt * 9 * CHANNELS
        t_buf[dt * 9 : dt * 9 + 9] = jnp.dot(
            w_buf[at : at + 9 * CHANNELS, :], p_buf[...], preferred_element_type=jnp.float32
        ).reshape(9, CHANNELS, OUT)
        pair_copy(dt).start()

    for i in (1, 2):

        @pl.when(receives[i])
        def _():
            halo(i).wait_recv()

    taps_of(2)

    for cb in range(SUB):
        first = cb * ROWS // LANES * LANES
        last = min(first + 3 * LANES, bt_ref.shape[1])
        row = lax.broadcasted_iota(jnp.int32, (last - first, ROWS), 0)
        col = lax.broadcasted_iota(jnp.int32, (last - first, ROWS), 1)
        wanted = cb * ROWS - first + lax.rem(col, SUB) * TAPS + col // SUB
        pick = jnp.where(row == wanted, 1.0, 0.0).astype(jnp.bfloat16)
        b_buf[cb] = jnp.dot(
            bt_ref[:, first:last], pick, preferred_element_type=jnp.float32
        ).astype(jnp.bfloat16)
    rot_buf[...] = jnp.zeros_like(rot_buf)

    @pl.when(receives[0])
    def _():
        halo(0).wait_recv()

    for i in (3, 4):

        @pl.when(sends[i])
        def _():
            halo(i).start()

    for i in (3, 4):

        @pl.when(receives[i])
        def _():
            halo(i).wait_recv()

    taps_of(1)
    taps_of(0)

    def plane_copy(d):
        return pltpu.make_async_remote_copy(
            src_ref=s_buf.at[d],
            dst_ref=r_buf.at[d],
            send_sem=s_send.at[d],
            recv_sem=s_recv.at[d],
            device_id={"height": lax.rem(me + d, CHIPS)},
            device_id_type=MESH,
        )

    def chunk(d):
        chip = lax.rem(me + d, CHIPS)
        low = chip // SUB
        rows = pl.ds(pl.multiple_of(lax.rem(chip, SUB) * SUB, SUB), SUB)
        own = t_buf[:, rows, pl.ds(pl.multiple_of((2 * core + low) * LANES, LANES), LANES)]
        other = c_buf[:, rows, pl.ds(pl.multiple_of(low * LANES, LANES), LANES)]
        return (own + other).reshape(ROWS, LANES)

    for dt in (2, 1, 0):
        pair_copy(dt).wait_recv()

    @pl.loop(1, CHIPS)
    def _(d):
        s_buf[d] = chunk(d).astype(jnp.bfloat16)
        plane_copy(d).start()

    acc[...] = chunk(0)

    @pl.loop(1, CHIPS)
    def _(d):
        plane_copy(d).wait_recv()
        acc[...] += r_buf[d].astype(jnp.float32)

    z_out[...] = acc[...].astype(jnp.bfloat16)
    z_copy = pltpu.make_async_remote_copy(
        src_ref=z_out,
        dst_ref=z_in,
        send_sem=z_send,
        recv_sem=z_recv,
        device_id={"tm": far},
        device_id_type=MESH,
    )
    z_copy.start()
    z_copy.wait_recv()

    def place(which, d):
        owner = lax.rem(me - d + CHIPS, CHIPS)
        return 2 * which + owner // SUB, lax.rem(owner, SUB)

    def gather_copy(d):
        kb, cb = place(core, 0)
        return pltpu.make_async_remote_copy(
            src_ref=g_buf.at[kb, cb],
            dst_ref=g_buf.at[kb, cb],
            send_sem=g_send.at[d],
            recv_sem=g_recv.at[d],
            device_id={"height": lax.rem(me + d, CHIPS)},
            device_id_type=MESH,
        )

    def hand_copy(d):
        kb, cb = place(core, d)
        return pltpu.make_async_remote_copy(
            src_ref=g_buf.at[kb, cb],
            dst_ref=g_buf.at[kb, cb],
            send_sem=f_send.at[d],
            recv_sem=f_recv.at[d],
            device_id={"tm": mate},
            device_id_type=MESH,
        )

    def rotate(which, d):
        kb, cb = place(which, d)
        rot_buf[kb] += jnp.dot(b_buf[cb], g_buf[kb, cb], preferred_element_type=jnp.float32)

    kb0, cb0 = place(core, 0)
    g_buf[kb0, cb0] = (acc[...] + z_in[...].astype(jnp.float32)).astype(jnp.bfloat16)

    @pl.loop(1, CHIPS)
    def _(d):
        gather_copy(d).start()

    hand_copy(0).start()
    rotate(core, 0)

    @pl.loop(1, CHIPS)
    def _(d):
        gather_copy(d).wait_recv()
        hand_copy(d).start()
        rotate(core, d)

    @pl.loop(0, CHIPS)
    def _(d):
        hand_copy(d).wait_recv()
        rotate(1 - core, d)

    for kb in range(4):
        fin_buf[2 * kb : 2 * kb + 2] = rot_buf[kb].T.reshape(2, CHANNELS, ROWS)

    def panel_copy(d):
        return pltpu.make_async_remote_copy(
            src_ref=q_buf.at[d],
            dst_ref=y_buf.at[d],
            send_sem=q_send.at[d],
            recv_sem=q_recv.at[d],
            device_id={"panel": lax.rem(panel + d, PANELS)},
            device_id_type=MESH,
        )

    @pl.loop(1, PANELS)
    def _(d):
        q_buf[d] = fin_buf[lax.rem(panel + d, PANELS)].astype(jnp.bfloat16)
        panel_copy(d).start()

    out_ref[...] = fin_buf[panel]

    @pl.loop(1, PANELS)
    def _(d):
        panel_copy(d).wait_recv()
        out_ref[...] += y_buf[d].astype(jnp.float32)

    out_ref[...] = out_ref[...] / (eig_ref[...] + damping)

    for i in range(5):

        @pl.when(sends[i])
        def _():
            halo(i).wait_send()

    for dt in range(3):
        pair_copy(dt).wait_send()
    z_copy.wait_send()
    hand_copy(0).wait_send()

    @pl.loop(1, CHIPS)
    def _(d):
        plane_copy(d).wait_send()
        gather_copy(d).wait_send()
        hand_copy(d).wait_send()

    @pl.loop(1, PANELS)
    def _(d):
        panel_copy(d).wait_send()


def body(activations, out_grad, out_basis, in_basis, eigenvalues, forget_order):
    dma = pltpu.SemaphoreType.DMA
    bf16, f32 = jnp.bfloat16, jnp.float32
    vmem = pl.BlockSpec(memory_space=pltpu.VMEM)
    positions = BLOCKS * LANES
    return pl.pallas_call(
        kernel,
        out_shape=jax.ShapeDtypeStruct(eigenvalues.shape, f32),
        in_specs=[pl.BlockSpec(memory_space=pltpu.SMEM)] + [vmem] * 5,
        out_specs=vmem,
        scratch_shapes=[
            pltpu.VMEM((FORGET, 4, 4, CHANNELS, LANES), bf16),
            pltpu.VMEM((TAPS * CHANNELS, positions), bf16),
            pltpu.VMEM((positions, OUT), bf16),
            pltpu.VMEM((TAPS, CHANNELS, OUT), f32),
            pltpu.VMEM((TAPS, CHANNELS, OUT // 2), f32),
            pltpu.VMEM((CHIPS, ROWS, LANES), bf16),
            pltpu.VMEM((CHIPS, ROWS, LANES), bf16),
            pltpu.VMEM((ROWS, LANES), f32),
            pltpu.VMEM((ROWS, LANES), bf16),
            pltpu.VMEM((ROWS, LANES), bf16),
            pltpu.VMEM((4, SUB, ROWS, LANES), bf16),
            pltpu.VMEM((SUB, ROWS, ROWS), bf16),
            pltpu.VMEM((4, ROWS, LANES), f32),
            pltpu.VMEM((PANELS, CHANNELS, ROWS), f32),
            pltpu.VMEM((PANELS, CHANNELS, ROWS), bf16),
            pltpu.VMEM((PANELS, CHANNELS, ROWS), bf16),
            dma((5,)),
            dma((5,)),
            dma((3,)),
            dma((3,)),
            dma((CHIPS,)),
            dma((CHIPS,)),
            dma(()),
            dma(()),
            dma((CHIPS,)),
            dma((CHIPS,)),
            dma((CHIPS,)),
            dma((CHIPS,)),
            dma((PANELS,)),
            dma((PANELS,)),
        ],
        compiler_params=pltpu.CompilerParams(
            collective_id=0, has_side_effects=True, vmem_limit_bytes=56 * 1024 * 1024
        ),
    )(forget_order, activations, out_grad, out_basis, in_basis.T, eigenvalues)


def solution(mesh):
    in_specs = (
        P(None, "tm", "height", "panel", None),
        P(None, "tm", "height", None, None),
        P(),
        P("panel", ("tm", "height")),
        P("panel", ("tm", "height")),
        P(),
    )
    out_specs = P("panel", ("tm", "height"))
    return jax.shard_map(body, mesh=mesh, in_specs=in_specs, out_specs=out_specs, check_vma=False)
```

```python
import jax
import jax.numpy as jnp
from jax import lax
from jax.experimental import pallas as pl
from jax.experimental.pallas import tpu as pltpu
from jax.sharding import PartitionSpec as P

FORGET = 3
TAPS = 27
LANES = 128
SUB = 8
SLABS = 4
CHIPS = 16
PANELS = 8
BLOCKS = 12
CHANNELS = 64
OUT = 512
ROWS = TAPS * SUB
PARTS = 3
PIECE = 9 * SUB
DEPTH = SUB * PIECE
MESH = pl.DeviceIdType.MESH


damping = 0.1


def kernel(
    order_ref,
    act_ref,
    grad_ref,
    ob_ref,
    bt_ref,
    eig_ref,
    out_ref,
    e_buf,
    w_buf,
    p_buf,
    t_buf,
    c_buf,
    s_buf,
    r_buf,
    acc,
    z_out,
    z_in,
    g_buf,
    m_buf,
    b_buf,
    rot_buf,
    fin_buf,
    q_buf,
    y_buf,
    h_send,
    h_recv,
    c_send,
    c_recv,
    s_send,
    s_recv,
    z_send,
    z_recv,
    g_send,
    g_recv,
    f_send,
    f_recv,
    q_send,
    q_recv,
):
    tm = lax.axis_index("tm")
    me = lax.axis_index("height")
    panel = lax.axis_index("panel")
    core = lax.rem(tm, 2)
    mate = tm + 1 - 2 * core
    far = lax.rem(tm + 2, SLABS)
    up = lax.rem(me + 1, CHIPS)
    down = lax.rem(me + CHIPS - 1, CHIPS)

    barrier = pltpu.get_barrier_semaphore()
    for axis, mine, count in (("tm", tm, SLABS), ("height", me, CHIPS), ("panel", panel, PANELS)):

        @pl.loop(1, count)
        def _(d):
            pl.semaphore_signal(
                barrier, inc=1, device_id={axis: lax.rem(mine + d, count)}, device_id_type=MESH
            )

    for n in range(FORGET):
        e_buf[n, 2:4, 1:3] = act_ref[order_ref[n]]

    @pl.when(tm == 0)
    def _():
        e_buf[:, 0:2] = jnp.zeros_like(e_buf[:, 0:2])

    @pl.when(me == 0)
    def _():
        e_buf[:, :, 0:1] = jnp.zeros_like(e_buf[:, :, 0:1])

    @pl.when(me == CHIPS - 1)
    def _():
        e_buf[:, :, 3:4] = jnp.zeros_like(e_buf[:, :, 3:4])

    def halo(i):
        source, target, device = (
            ((slice(2, 4), slice(1, 3)), (slice(0, 2), slice(1, 3)), {"tm": lax.rem(tm + 1, SLABS)}),
            ((slice(2, 4), slice(2, 3)), (slice(2, 4), slice(0, 1)), {"height": up}),
            ((slice(2, 4), slice(1, 2)), (slice(2, 4), slice(3, 4)), {"height": down}),
            ((slice(0, 2), slice(2, 3)), (slice(0, 2), slice(0, 1)), {"height": up}),
            ((slice(0, 2), slice(1, 2)), (slice(0, 2), slice(3, 4)), {"height": down}),
        )[i]
        return pltpu.make_async_remote_copy(
            src_ref=e_buf.at[(slice(None),) + source],
            dst_ref=e_buf.at[(slice(None),) + target],
            send_sem=h_send.at[i],
            recv_sem=h_recv.at[i],
            device_id=device,
            device_id_type=MESH,
        )

    sends = (
        tm < SLABS - 1,
        me < CHIPS - 1,
        me > 0,
        jnp.logical_and(tm > 0, me < CHIPS - 1),
        jnp.logical_and(tm > 0, me > 0),
    )
    receives = (
        tm > 0,
        me > 0,
        me < CHIPS - 1,
        jnp.logical_and(tm > 0, me > 0),
        jnp.logical_and(tm > 0, me < CHIPS - 1),
    )

    @pl.loop(0, BLOCKS)
    def _(b):
        block = grad_ref[order_ref[b // 4], lax.rem(b // 2, 2), lax.rem(b, 2)]
        rows = pl.ds(pl.multiple_of(b * LANES, LANES), LANES)
        p_buf[rows, :] = lax.dot_general(
            block, ob_ref[...], (((0,), (0,)), ((), ())), preferred_element_type=jnp.float32
        ).astype(jnp.bfloat16)

    pl.semaphore_wait(barrier, SLABS + CHIPS + PANELS - 3)
    for i in range(3):

        @pl.when(sends[i])
        def _():
            halo(i).start()

    def half(which):
        return pl.ds(pl.multiple_of(which * 2 * LANES, 2 * LANES), 2 * LANES)

    def pair_copy(dt):
        return pltpu.make_async_remote_copy(
            src_ref=t_buf.at[pl.ds(dt * 9, 9), :, half(1 - core)],
            dst_ref=c_buf.at[pl.ds(dt * 9, 9)],
            send_sem=c_send.at[dt],
            recv_sem=c_recv.at[dt],
            device_id={"tm": mate},
            device_id_type=MESH,
        )

    column = lax.broadcasted_iota(jnp.int32, (CHANNELS, LANES), 1)

    def taps_of(dt):
        @pl.loop(0, BLOCKS)
        def _(b):
            n, f, r = b // 4, lax.rem(b // 2, 2), lax.rem(b, 2)
            lanes = pl.ds(pl.multiple_of(b * LANES, LANES), LANES)
            for dh in range(3):
                tile = e_buf[n, f + dt, r + dh]
                wide = tile.astype(jnp.float32)
                left = jnp.where(column == 0, 0.0, pltpu.roll(wide, 1, 1)).astype(jnp.bfloat16)
                right = jnp.where(column == LANES - 1, 0.0, pltpu.roll(wide, LANES - 1, 1)).astype(
                    jnp.bfloat16
                )
                for dw, shifted in enumerate((left, tile, right)):
                    at = (dt * 9 + dh * 3 + dw) * CHANNELS
                    w_buf[at : at + CHANNELS, lanes] = shifted

        at = dt * 9 * CHANNELS
        t_buf[dt * 9 : dt * 9 + 9] = jnp.dot(
            w_buf[at : at + 9 * CHANNELS, :], p_buf[...], preferred_element_type=jnp.float32
        ).reshape(9, CHANNELS, OUT)
        pair_copy(dt).start()

    for i in (1, 2):

        @pl.when(receives[i])
        def _():
            halo(i).wait_recv()

    taps_of(2)

    for cb in range(SUB):
        first = cb * ROWS // LANES * LANES
        last = min(first + 3 * LANES, bt_ref.shape[1])
        row = lax.broadcasted_iota(jnp.int32, (ROWS, last - first), 0)
        col = lax.broadcasted_iota(jnp.int32, (ROWS, last - first), 1)
        wanted = cb * ROWS - first + lax.rem(row, SUB) * TAPS + row // SUB
        pick = jnp.where(col == wanted, 1.0, 0.0).astype(jnp.bfloat16)
        moved = lax.dot_general(
            pick,
            bt_ref[:, first:last],
            (((1,), (1,)), ((), ())),
            preferred_element_type=jnp.float32,
        )
        for p in range(PARTS):
            m_buf[p, cb * PIECE : (cb + 1) * PIECE, :] = moved[p * PIECE : (p + 1) * PIECE]
    for p in range(PARTS):
        b_buf[p] = m_buf[p].T.astype(jnp.bfloat16)
    rot_buf[...] = jnp.zeros_like(rot_buf)

    def plane_copy(p, d):
        return pltpu.make_async_remote_copy(
            src_ref=s_buf.at[p, d],
            dst_ref=r_buf.at[p, d],
            send_sem=s_send.at[p, d],
            recv_sem=s_recv.at[p, d],
            device_id={"height": lax.rem(me + d, CHIPS)},
            device_id_type=MESH,
        )

    def chunk(p, d):
        chip = lax.rem(me + d, CHIPS)
        low = chip // SUB
        taps = pl.ds(9 * p, 9)
        rows = pl.ds(pl.multiple_of(lax.rem(chip, SUB) * SUB, SUB), SUB)
        own = t_buf[taps, rows, pl.ds(pl.multiple_of((2 * core + low) * LANES, LANES), LANES)]
        other = c_buf[taps, rows, pl.ds(pl.multiple_of(low * LANES, LANES), LANES)]
        return (own + other).reshape(PIECE, LANES)

    def plane_start(p):
        pair_copy(p).wait_recv()

        @pl.loop(1, CHIPS)
        def _(d):
            s_buf[p, d] = chunk(p, d).astype(jnp.bfloat16)
            plane_copy(p, d).start()

        acc[p] = chunk(p, 0)

    def z_copy(p):
        return pltpu.make_async_remote_copy(
            src_ref=z_out.at[p],
            dst_ref=z_in.at[p],
            send_sem=z_send.at[p],
            recv_sem=z_recv.at[p],
            device_id={"tm": far},
            device_id_type=MESH,
        )

    def plane_finish(p):
        @pl.loop(1, CHIPS)
        def _(d):
            plane_copy(p, d).wait_recv()
            acc[p] += r_buf[p, d].astype(jnp.float32)

        z_out[p] = acc[p].astype(jnp.bfloat16)
        z_copy(p).start()

    def place(d):
        owner = lax.rem(me - d + CHIPS, CHIPS)
        return 2 * core + owner // SUB, lax.rem(owner, SUB)

    def gather_copy(p, d):
        kb, cb = place(0)
        return pltpu.make_async_remote_copy(
            src_ref=g_buf.at[p, kb, cb],
            dst_ref=g_buf.at[p, kb, cb],
            send_sem=g_send.at[p, d],
            recv_sem=g_recv.at[p, d],
            device_id={"height": lax.rem(me + d, CHIPS)},
            device_id_type=MESH,
        )

    def hand_copy(p, d):
        kb, cb = place(d)
        return pltpu.make_async_remote_copy(
            src_ref=g_buf.at[p, kb, cb],
            dst_ref=g_buf.at[p, kb, cb],
            send_sem=f_send.at[p, d],
            recv_sem=f_recv.at[p, d],
            device_id={"tm": mate},
            device_id_type=MESH,
        )

    def z_finish(p):
        z_copy(p).wait_recv()
        kb, cb = place(0)
        g_buf[p, kb, cb] = (acc[p] + z_in[p].astype(jnp.float32)).astype(jnp.bfloat16)

        @pl.loop(1, CHIPS)
        def _(d):
            gather_copy(p, d).start()

        hand_copy(p, 0).start()

    def rotate(which, p):
        sides = [
            g_buf[p, 2 * which + i].astype(jnp.float32).reshape(DEPTH, LANES).astype(jnp.bfloat16)
            for i in range(2)
        ]
        rot_buf[which] += jnp.dot(
            b_buf[p], jnp.concatenate(sides, axis=1), preferred_element_type=jnp.float32
        )

    def gather_finish(p):
        @pl.loop(1, CHIPS)
        def _(d):
            gather_copy(p, d).wait_recv()
            hand_copy(p, d).start()

        rotate(core, p)

    def hand_finish(p):
        @pl.loop(0, CHIPS)
        def _(d):
            hand_copy(p, d).wait_recv()

        rotate(1 - core, p)

    def panel_copy(d):
        return pltpu.make_async_remote_copy(
            src_ref=q_buf.at[d],
            dst_ref=y_buf.at[d],
            send_sem=q_send.at[d],
            recv_sem=q_recv.at[d],
            device_id={"panel": lax.rem(panel + d, PANELS)},
            device_id_type=MESH,
        )

    def panel_start(which):
        fin_buf[pl.ds(4 * which, 4)] = rot_buf[which].T.reshape(4, CHANNELS, ROWS)

        @pl.loop(0, 4)
        def _(i):
            target = 4 * which + i

            @pl.when(target != panel)
            def _():
                d = lax.rem(target - panel + PANELS, PANELS)
                q_buf[d] = fin_buf[target].astype(jnp.bfloat16)
                panel_copy(d).start()

    @pl.when(receives[0])
    def _():
        halo(0).wait_recv()

    for i in (3, 4):

        @pl.when(sends[i])
        def _():
            halo(i).start()

    plane_start(2)

    for i in (3, 4):

        @pl.when(receives[i])
        def _():
            halo(i).wait_recv()

    taps_of(1)
    plane_finish(2)
    taps_of(0)
    plane_start(1)
    plane_start(0)
    plane_finish(1)
    z_finish(2)
    plane_finish(0)
    z_finish(1)
    gather_finish(2)
    hand_finish(2)
    z_finish(0)
    gather_finish(1)
    hand_finish(1)
    gather_finish(0)
    panel_start(core)
    hand_finish(0)
    panel_start(1 - core)

    out_ref[...] = fin_buf[panel]

    @pl.loop(1, PANELS)
    def _(d):
        panel_copy(d).wait_recv()
        out_ref[...] += y_buf[d].astype(jnp.float32)

    out_ref[...] = out_ref[...] / (eig_ref[...] + damping)

    for i in range(5):

        @pl.when(sends[i])
        def _():
            halo(i).wait_send()

    for p in range(PARTS):
        pair_copy(p).wait_send()
        z_copy(p).wait_send()
        hand_copy(p, 0).wait_send()

        @pl.loop(1, CHIPS)
        def _(d):
            plane_copy(p, d).wait_send()
            gather_copy(p, d).wait_send()
            hand_copy(p, d).wait_send()

    @pl.loop(1, PANELS)
    def _(d):
        panel_copy(d).wait_send()


def body(activations, out_grad, out_basis, in_basis, eigenvalues, forget_order):
    dma = pltpu.SemaphoreType.DMA
    bf16, f32 = jnp.bfloat16, jnp.float32
    vmem = pl.BlockSpec(memory_space=pltpu.VMEM)
    positions = BLOCKS * LANES
    return pl.pallas_call(
        kernel,
        out_shape=jax.ShapeDtypeStruct(eigenvalues.shape, f32),
        in_specs=[pl.BlockSpec(memory_space=pltpu.SMEM)] + [vmem] * 5,
        out_specs=vmem,
        scratch_shapes=[
            pltpu.VMEM((FORGET, 4, 4, CHANNELS, LANES), bf16),
            pltpu.VMEM((TAPS * CHANNELS, positions), bf16),
            pltpu.VMEM((positions, OUT), bf16),
            pltpu.VMEM((TAPS, CHANNELS, OUT), f32),
            pltpu.VMEM((TAPS, CHANNELS, OUT // 2), f32),
            pltpu.VMEM((PARTS, CHIPS, PIECE, LANES), bf16),
            pltpu.VMEM((PARTS, CHIPS, PIECE, LANES), bf16),
            pltpu.VMEM((PARTS, PIECE, LANES), f32),
            pltpu.VMEM((PARTS, PIECE, LANES), bf16),
            pltpu.VMEM((PARTS, PIECE, LANES), bf16),
            pltpu.VMEM((PARTS, 4, SUB, PIECE, LANES), bf16),
            pltpu.VMEM((PARTS, DEPTH, ROWS), f32),
            pltpu.VMEM((PARTS, ROWS, DEPTH), bf16),
            pltpu.VMEM((2, ROWS, 2 * LANES), f32),
            pltpu.VMEM((PANELS, CHANNELS, ROWS), f32),
            pltpu.VMEM((PANELS, CHANNELS, ROWS), bf16),
            pltpu.VMEM((PANELS, CHANNELS, ROWS), bf16),
            dma((5,)),
            dma((5,)),
            dma((3,)),
            dma((3,)),
            dma((PARTS, CHIPS)),
            dma((PARTS, CHIPS)),
            dma((PARTS,)),
            dma((PARTS,)),
            dma((PARTS, CHIPS)),
            dma((PARTS, CHIPS)),
            dma((PARTS, CHIPS)),
            dma((PARTS, CHIPS)),
            dma((PANELS,)),
            dma((PANELS,)),
        ],
        compiler_params=pltpu.CompilerParams(
            collective_id=0, has_side_effects=True, vmem_limit_bytes=56 * 1024 * 1024
        ),
    )(forget_order, activations, out_grad, out_basis, in_basis.T, eigenvalues)


def solution(mesh):
    in_specs = (
        P(None, "tm", "height", "panel", None),
        P(None, "tm", "height", None, None),
        P(),
        P("panel", ("tm", "height")),
        P("panel", ("tm", "height")),
        P(),
    )
    out_specs = P("panel", ("tm", "height"))
    return jax.shard_map(body, mesh=mesh, in_specs=in_specs, out_specs=out_specs, check_vma=False)
```

```python
import jax
import jax.numpy as jnp
from jax import lax
from jax.experimental import pallas as pl
from jax.experimental.pallas import tpu as pltpu
from jax.sharding import PartitionSpec as P

FORGET = 3
TAPS = 27
LANES = 128
SUB = 8
SLABS = 4
CHIPS = 16
PANELS = 8
BLOCKS = 12
CHANNELS = 64
OUT = 512
ROWS = TAPS * SUB
PARTS = 3
PIECE = 9 * SUB
DEPTH = SUB * PIECE
MESH = pl.DeviceIdType.MESH


damping = 0.1


def kernel(
    order_ref,
    act_in,
    grad_in,
    ob_in,
    bt_in,
    eig_in,
    out_ref,
    act_ref,
    grad_ref,
    ob_ref,
    bt_ref,
    eig_ref,
    in_sem,
    e_buf,
    w_buf,
    p_buf,
    t_buf,
    c_buf,
    s_buf,
    r_buf,
    acc,
    z_out,
    z_in,
    g_buf,
    m_buf,
    b_buf,
    rot_buf,
    fin_buf,
    q_buf,
    y_buf,
    h_send,
    h_recv,
    c_send,
    c_recv,
    s_send,
    s_recv,
    z_send,
    z_recv,
    g_send,
    g_recv,
    f_send,
    f_recv,
    q_send,
    q_recv,
):
    tm = lax.axis_index("tm")
    me = lax.axis_index("height")
    panel = lax.axis_index("panel")
    core = lax.rem(tm, 2)
    mate = tm + 1 - 2 * core
    far = lax.rem(tm + 2, SLABS)
    up = lax.rem(me + 1, CHIPS)
    down = lax.rem(me + CHIPS - 1, CHIPS)

    barrier = pltpu.get_barrier_semaphore()
    for axis, mine, count in (("tm", tm, SLABS), ("height", me, CHIPS), ("panel", panel, PANELS)):

        @pl.loop(1, count)
        def _(d):
            pl.semaphore_signal(
                barrier, inc=1, device_id={axis: lax.rem(mine + d, count)}, device_id_type=MESH
            )

    loads = [
        pltpu.make_async_copy(source, target, in_sem.at[i])
        for i, (source, target) in enumerate(
            (
                (act_in, act_ref),
                (ob_in, ob_ref),
                (grad_in, grad_ref),
                (bt_in, bt_ref),
                (eig_in, eig_ref),
            )
        )
    ]
    for load in loads:
        load.start()
    loads[0].wait()

    for n in range(FORGET):
        e_buf[n, 2:4, 1:3] = act_ref[order_ref[n]]

    @pl.when(tm == 0)
    def _():
        e_buf[:, 0:2] = jnp.zeros_like(e_buf[:, 0:2])

    @pl.when(me == 0)
    def _():
        e_buf[:, :, 0:1] = jnp.zeros_like(e_buf[:, :, 0:1])

    @pl.when(me == CHIPS - 1)
    def _():
        e_buf[:, :, 3:4] = jnp.zeros_like(e_buf[:, :, 3:4])

    def halo(i):
        source, target, device = (
            ((slice(2, 4), slice(1, 3)), (slice(0, 2), slice(1, 3)), {"tm": lax.rem(tm + 1, SLABS)}),
            ((slice(2, 4), slice(2, 3)), (slice(2, 4), slice(0, 1)), {"height": up}),
            ((slice(2, 4), slice(1, 2)), (slice(2, 4), slice(3, 4)), {"height": down}),
            ((slice(0, 2), slice(2, 3)), (slice(0, 2), slice(0, 1)), {"height": up}),
            ((slice(0, 2), slice(1, 2)), (slice(0, 2), slice(3, 4)), {"height": down}),
        )[i]
        return pltpu.make_async_remote_copy(
            src_ref=e_buf.at[(slice(None),) + source],
            dst_ref=e_buf.at[(slice(None),) + target],
            send_sem=h_send.at[i],
            recv_sem=h_recv.at[i],
            device_id=device,
            device_id_type=MESH,
        )

    sends = (
        tm < SLABS - 1,
        me < CHIPS - 1,
        me > 0,
        jnp.logical_and(tm > 0, me < CHIPS - 1),
        jnp.logical_and(tm > 0, me > 0),
    )
    receives = (
        tm > 0,
        me > 0,
        me < CHIPS - 1,
        jnp.logical_and(tm > 0, me > 0),
        jnp.logical_and(tm > 0, me < CHIPS - 1),
    )

    pl.semaphore_wait(barrier, SLABS + CHIPS + PANELS - 3)
    for i in range(3):

        @pl.when(sends[i])
        def _():
            halo(i).start()

    loads[1].wait()
    loads[2].wait()

    @pl.loop(0, BLOCKS)
    def _(b):
        block = grad_ref[order_ref[b // 4], lax.rem(b // 2, 2), lax.rem(b, 2)]
        rows = pl.ds(pl.multiple_of(b * LANES, LANES), LANES)
        p_buf[rows, :] = lax.dot_general(
            block, ob_ref[...], (((0,), (0,)), ((), ())), preferred_element_type=jnp.float32
        ).astype(jnp.bfloat16)

    def half(which):
        return pl.ds(pl.multiple_of(which * 2 * LANES, 2 * LANES), 2 * LANES)

    def pair_copy(dt):
        return pltpu.make_async_remote_copy(
            src_ref=t_buf.at[pl.ds(dt * 9, 9), :, half(1 - core)],
            dst_ref=c_buf.at[pl.ds(dt * 9, 9)],
            send_sem=c_send.at[dt],
            recv_sem=c_recv.at[dt],
            device_id={"tm": mate},
            device_id_type=MESH,
        )

    column = lax.broadcasted_iota(jnp.int32, (CHANNELS, LANES), 1)

    def windows(e):
        @pl.loop(0, FORGET)
        def _(n):
            for q in range(4):
                tile = e_buf[n, e, q]
                wide = tile.astype(jnp.float32)
                left = jnp.where(column == 0, 0.0, pltpu.roll(wide, 1, 1)).astype(jnp.bfloat16)
                right = jnp.where(column == LANES - 1, 0.0, pltpu.roll(wide, LANES - 1, 1)).astype(
                    jnp.bfloat16
                )
                for f in range(2):
                    for r in range(2):
                        dt, dh = e - f, q - r
                        if not (0 <= dt < 3 and 0 <= dh < 3):
                            continue
                        lanes = pl.ds(
                            pl.multiple_of(n * 4 * LANES, LANES) + (f * 2 + r) * LANES, LANES
                        )
                        for dw, shifted in enumerate((left, tile, right)):
                            at = (dt * 9 + dh * 3 + dw) * CHANNELS
                            w_buf[at : at + CHANNELS, lanes] = shifted

    def taps_of(dt):
        at = dt * 9 * CHANNELS
        t_buf[dt * 9 : dt * 9 + 9] = jnp.dot(
            w_buf[at : at + 9 * CHANNELS, :], p_buf[...], preferred_element_type=jnp.float32
        ).reshape(9, CHANNELS, OUT)
        pair_copy(dt).start()

    for i in (1, 2):

        @pl.when(receives[i])
        def _():
            halo(i).wait_recv()

    windows(2)
    windows(3)
    taps_of(2)

    def plane_copy(p, d):
        return pltpu.make_async_remote_copy(
            src_ref=s_buf.at[p, d],
            dst_ref=r_buf.at[p, d],
            send_sem=s_send.at[p, d],
            recv_sem=s_recv.at[p, d],
            device_id={"height": lax.rem(me + d, CHIPS)},
            device_id_type=MESH,
        )

    def chunk(p, d):
        chip = lax.rem(me + d, CHIPS)
        low = chip // SUB
        taps = pl.ds(9 * p, 9)
        rows = pl.ds(pl.multiple_of(lax.rem(chip, SUB) * SUB, SUB), SUB)
        own = t_buf[taps, rows, pl.ds(pl.multiple_of((2 * core + low) * LANES, LANES), LANES)]
        other = c_buf[taps, rows, pl.ds(pl.multiple_of(low * LANES, LANES), LANES)]
        return (own + other).reshape(PIECE, LANES)

    def plane_start(p):
        pair_copy(p).wait_recv()

        @pl.loop(1, CHIPS)
        def _(d):
            s_buf[p, d] = chunk(p, d).astype(jnp.bfloat16)
            plane_copy(p, d).start()

        acc[p] = chunk(p, 0)

    def z_copy(p):
        return pltpu.make_async_remote_copy(
            src_ref=z_out.at[p],
            dst_ref=z_in.at[p],
            send_sem=z_send.at[p],
            recv_sem=z_recv.at[p],
            device_id={"tm": far},
            device_id_type=MESH,
        )

    def plane_finish(p):
        @pl.loop(1, CHIPS)
        def _(d):
            plane_copy(p, d).wait_recv()
            acc[p] += r_buf[p, d].astype(jnp.float32)

        z_out[p] = acc[p].astype(jnp.bfloat16)
        z_copy(p).start()

    def place(d):
        owner = lax.rem(me - d + CHIPS, CHIPS)
        return 2 * core + owner // SUB, lax.rem(owner, SUB)

    def gather_copy(p, d):
        kb, cb = place(0)
        return pltpu.make_async_remote_copy(
            src_ref=g_buf.at[p, kb, cb],
            dst_ref=g_buf.at[p, kb, cb],
            send_sem=g_send.at[p, d],
            recv_sem=g_recv.at[p, d],
            device_id={"height": lax.rem(me + d, CHIPS)},
            device_id_type=MESH,
        )

    def hand_copy(p, d):
        kb, cb = place(d)
        return pltpu.make_async_remote_copy(
            src_ref=g_buf.at[p, kb, cb],
            dst_ref=g_buf.at[p, kb, cb],
            send_sem=f_send.at[p, d],
            recv_sem=f_recv.at[p, d],
            device_id={"tm": mate},
            device_id_type=MESH,
        )

    def z_finish(p):
        z_copy(p).wait_recv()
        kb, cb = place(0)
        g_buf[p, kb, cb] = (acc[p] + z_in[p].astype(jnp.float32)).astype(jnp.bfloat16)

        @pl.loop(1, CHIPS)
        def _(d):
            gather_copy(p, d).start()

        hand_copy(p, 0).start()

    def rotate(which, p):
        sides = [
            g_buf[p, 2 * which + i].astype(jnp.float32).reshape(DEPTH, LANES).astype(jnp.bfloat16)
            for i in range(2)
        ]
        rot_buf[which] += jnp.dot(
            b_buf[p], jnp.concatenate(sides, axis=1), preferred_element_type=jnp.float32
        )

    def gather_finish(p):
        @pl.loop(1, CHIPS)
        def _(d):
            gather_copy(p, d).wait_recv()
            hand_copy(p, d).start()

        rotate(core, p)

    def hand_finish(p):
        @pl.loop(0, CHIPS)
        def _(d):
            hand_copy(p, d).wait_recv()

        rotate(1 - core, p)

    def panel_copy(d):
        return pltpu.make_async_remote_copy(
            src_ref=q_buf.at[d],
            dst_ref=y_buf.at[d],
            send_sem=q_send.at[d],
            recv_sem=q_recv.at[d],
            device_id={"panel": lax.rem(panel + d, PANELS)},
            device_id_type=MESH,
        )

    def panel_start(which):
        fin_buf[pl.ds(4 * which, 4)] = rot_buf[which].T.reshape(4, CHANNELS, ROWS)

        @pl.loop(0, 4)
        def _(i):
            target = 4 * which + i

            @pl.when(target != panel)
            def _():
                d = lax.rem(target - panel + PANELS, PANELS)
                q_buf[d] = fin_buf[target].astype(jnp.bfloat16)
                panel_copy(d).start()

    @pl.when(receives[0])
    def _():
        halo(0).wait_recv()

    for i in (3, 4):

        @pl.when(sends[i])
        def _():
            halo(i).start()

    for i in (3, 4):

        @pl.when(receives[i])
        def _():
            halo(i).wait_recv()

    windows(1)
    plane_start(2)
    taps_of(1)
    windows(0)
    plane_start(1)
    taps_of(0)
    plane_finish(2)
    plane_start(0)
    plane_finish(1)

    loads[3].wait()
    loads[4].wait()

    for cb in range(SUB):
        first = cb * ROWS // LANES * LANES
        last = min(first + 3 * LANES, bt_ref.shape[1])
        row = lax.broadcasted_iota(jnp.int32, (ROWS, last - first), 0)
        col = lax.broadcasted_iota(jnp.int32, (ROWS, last - first), 1)
        wanted = cb * ROWS - first + lax.rem(row, SUB) * TAPS + row // SUB
        pick = jnp.where(col == wanted, 1.0, 0.0).astype(jnp.bfloat16)
        moved = lax.dot_general(
            pick,
            bt_ref[:, first:last],
            (((1,), (1,)), ((), ())),
            preferred_element_type=jnp.float32,
        )
        for p in range(PARTS):
            m_buf[p, cb * PIECE : (cb + 1) * PIECE, :] = moved[p * PIECE : (p + 1) * PIECE]
    for p in range(PARTS):
        b_buf[p] = m_buf[p].T.astype(jnp.bfloat16)
    rot_buf[...] = jnp.zeros_like(rot_buf)

    z_finish(2)
    plane_finish(0)
    z_finish(1)
    gather_finish(2)
    hand_finish(2)
    z_finish(0)
    gather_finish(1)
    hand_finish(1)
    gather_finish(0)
    panel_start(core)
    hand_finish(0)
    panel_start(1 - core)

    out_ref[...] = fin_buf[panel]

    @pl.loop(1, PANELS)
    def _(d):
        panel_copy(d).wait_recv()
        out_ref[...] += y_buf[d].astype(jnp.float32)

    out_ref[...] = out_ref[...] / (eig_ref[...] + damping)

    for i in range(5):

        @pl.when(sends[i])
        def _():
            halo(i).wait_send()

    for p in range(PARTS):
        pair_copy(p).wait_send()
        z_copy(p).wait_send()
        hand_copy(p, 0).wait_send()

        @pl.loop(1, CHIPS)
        def _(d):
            plane_copy(p, d).wait_send()
            gather_copy(p, d).wait_send()
            hand_copy(p, d).wait_send()

    @pl.loop(1, PANELS)
    def _(d):
        panel_copy(d).wait_send()


def body(activations, out_grad, out_basis, in_basis, eigenvalues, forget_order):
    dma = pltpu.SemaphoreType.DMA
    bf16, f32 = jnp.bfloat16, jnp.float32
    vmem = pl.BlockSpec(memory_space=pltpu.VMEM)
    positions = BLOCKS * LANES
    return pl.pallas_call(
        kernel,
        out_shape=jax.ShapeDtypeStruct(eigenvalues.shape, f32),
        in_specs=[pl.BlockSpec(memory_space=pltpu.SMEM)] + [pl.BlockSpec(memory_space=pl.ANY)] * 5,
        out_specs=vmem,
        scratch_shapes=[
            pltpu.VMEM(activations.shape, bf16),
            pltpu.VMEM(out_grad.shape, bf16),
            pltpu.VMEM(out_basis.shape, bf16),
            pltpu.VMEM(in_basis.shape[::-1], bf16),
            pltpu.VMEM(eigenvalues.shape, f32),
            dma((5,)),
            pltpu.VMEM((FORGET, 4, 4, CHANNELS, LANES), bf16),
            pltpu.VMEM((TAPS * CHANNELS, positions), bf16),
            pltpu.VMEM((positions, OUT), bf16),
            pltpu.VMEM((TAPS, CHANNELS, OUT), f32),
            pltpu.VMEM((TAPS, CHANNELS, OUT // 2), f32),
            pltpu.VMEM((PARTS, CHIPS, PIECE, LANES), bf16),
            pltpu.VMEM((PARTS, CHIPS, PIECE, LANES), bf16),
            pltpu.VMEM((PARTS, PIECE, LANES), f32),
            pltpu.VMEM((PARTS, PIECE, LANES), bf16),
            pltpu.VMEM((PARTS, PIECE, LANES), bf16),
            pltpu.VMEM((PARTS, 4, SUB, PIECE, LANES), bf16),
            pltpu.VMEM((PARTS, DEPTH, ROWS), f32),
            pltpu.VMEM((PARTS, ROWS, DEPTH), bf16),
            pltpu.VMEM((2, ROWS, 2 * LANES), f32),
            pltpu.VMEM((PANELS, CHANNELS, ROWS), f32),
            pltpu.VMEM((PANELS, CHANNELS, ROWS), bf16),
            pltpu.VMEM((PANELS, CHANNELS, ROWS), bf16),
            dma((5,)),
            dma((5,)),
            dma((3,)),
            dma((3,)),
            dma((PARTS, CHIPS)),
            dma((PARTS, CHIPS)),
            dma((PARTS,)),
            dma((PARTS,)),
            dma((PARTS, CHIPS)),
            dma((PARTS, CHIPS)),
            dma((PARTS, CHIPS)),
            dma((PARTS, CHIPS)),
            dma((PANELS,)),
            dma((PANELS,)),
        ],
        compiler_params=pltpu.CompilerParams(
            collective_id=0, has_side_effects=True, vmem_limit_bytes=56 * 1024 * 1024
        ),
    )(forget_order, activations, out_grad, out_basis, in_basis.T, eigenvalues)


def solution(mesh):
    in_specs = (
        P(None, "tm", "height", "panel", None),
        P(None, "tm", "height", None, None),
        P(),
        P("panel", ("tm", "height")),
        P("panel", ("tm", "height")),
        P(),
    )
    out_specs = P("panel", ("tm", "height"))
    return jax.shard_map(body, mesh=mesh, in_specs=in_specs, out_specs=out_specs, check_vma=False)
```

```python
import jax
import jax.numpy as jnp
from jax import lax
from jax.experimental import pallas as pl
from jax.experimental.pallas import tpu as pltpu
from jax.sharding import PartitionSpec as P

FORGET = 3
TAPS = 27
LANES = 128
SUB = 8
SLABS = 4
CHIPS = 16
PANELS = 8
BLOCKS = 12
CHANNELS = 64
OUT = 512
ROWS = TAPS * SUB
PARTS = 3
PIECE = 9 * SUB
DEPTH = SUB * PIECE
MESH = pl.DeviceIdType.MESH


damping = 0.1


def kernel(
    order_ref,
    act_in,
    grad_in,
    ob_in,
    bt_in,
    eig_in,
    out_ref,
    act_ref,
    grad_ref,
    ob_ref,
    bt_ref,
    eig_ref,
    in_sem,
    e_buf,
    w_buf,
    p_buf,
    t_buf,
    c_buf,
    s_buf,
    r_buf,
    acc,
    z_out,
    z_in,
    g_buf,
    m_buf,
    b_buf,
    rot_buf,
    fin_buf,
    q_buf,
    y_buf,
    h_send,
    h_recv,
    c_send,
    c_recv,
    s_send,
    s_recv,
    z_send,
    z_recv,
    g_send,
    g_recv,
    f_send,
    f_recv,
    q_send,
    q_recv,
):
    tm = lax.axis_index("tm")
    me = lax.axis_index("height")
    panel = lax.axis_index("panel")
    core = lax.rem(tm, 2)
    mate = tm + 1 - 2 * core
    far = lax.rem(tm + 2, SLABS)
    up = lax.rem(me + 1, CHIPS)
    down = lax.rem(me + CHIPS - 1, CHIPS)

    barrier = pltpu.get_barrier_semaphore()
    for axis, mine, count in (("tm", tm, SLABS), ("height", me, CHIPS), ("panel", panel, PANELS)):

        @pl.loop(1, count)
        def _(d):
            pl.semaphore_signal(
                barrier, inc=1, device_id={axis: lax.rem(mine + d, count)}, device_id_type=MESH
            )

    loads = [
        pltpu.make_async_copy(source, target, in_sem.at[i])
        for i, (source, target) in enumerate(
            (
                (act_in, act_ref),
                (ob_in, ob_ref),
                (grad_in, grad_ref),
                (bt_in, bt_ref),
                (eig_in, eig_ref),
            )
        )
    ]
    for load in loads:
        load.start()
    loads[0].wait()

    for n in range(FORGET):
        e_buf[n, 2:4, 1:3] = act_ref[order_ref[n]]

    @pl.when(tm == 0)
    def _():
        e_buf[:, 0:2] = jnp.zeros_like(e_buf[:, 0:2])

    @pl.when(me == 0)
    def _():
        e_buf[:, :, 0:1] = jnp.zeros_like(e_buf[:, :, 0:1])

    @pl.when(me == CHIPS - 1)
    def _():
        e_buf[:, :, 3:4] = jnp.zeros_like(e_buf[:, :, 3:4])

    def halo(i):
        source, target, device = (
            ((slice(2, 4), slice(1, 3)), (slice(0, 2), slice(1, 3)), {"tm": lax.rem(tm + 1, SLABS)}),
            ((slice(2, 4), slice(2, 3)), (slice(2, 4), slice(0, 1)), {"height": up}),
            ((slice(2, 4), slice(1, 2)), (slice(2, 4), slice(3, 4)), {"height": down}),
            ((slice(0, 2), slice(2, 3)), (slice(0, 2), slice(0, 1)), {"height": up}),
            ((slice(0, 2), slice(1, 2)), (slice(0, 2), slice(3, 4)), {"height": down}),
        )[i]
        return pltpu.make_async_remote_copy(
            src_ref=e_buf.at[(slice(None),) + source],
            dst_ref=e_buf.at[(slice(None),) + target],
            send_sem=h_send.at[i],
            recv_sem=h_recv.at[i],
            device_id=device,
            device_id_type=MESH,
        )

    sends = (
        tm < SLABS - 1,
        me < CHIPS - 1,
        me > 0,
        jnp.logical_and(tm > 0, me < CHIPS - 1),
        jnp.logical_and(tm > 0, me > 0),
    )
    receives = (
        tm > 0,
        me > 0,
        me < CHIPS - 1,
        jnp.logical_and(tm > 0, me > 0),
        jnp.logical_and(tm > 0, me < CHIPS - 1),
    )

    pl.semaphore_wait(barrier, SLABS + CHIPS + PANELS - 3)
    for i in range(3):

        @pl.when(sends[i])
        def _():
            halo(i).start()

    loads[1].wait()
    loads[2].wait()

    @pl.loop(0, BLOCKS)
    def _(b):
        block = grad_ref[order_ref[b // 4], lax.rem(b // 2, 2), lax.rem(b, 2)]
        rows = pl.ds(pl.multiple_of(b * LANES, LANES), LANES)
        p_buf[rows, :] = lax.dot_general(
            block, ob_ref[...], (((0,), (0,)), ((), ())), preferred_element_type=jnp.float32
        ).astype(jnp.bfloat16)

    def half(which):
        return pl.ds(pl.multiple_of(which * 2 * LANES, 2 * LANES), 2 * LANES)

    def pair_copy(dt):
        return pltpu.make_async_remote_copy(
            src_ref=t_buf.at[pl.ds(dt * 9, 9), :, half(1 - core)],
            dst_ref=c_buf.at[pl.ds(dt * 9, 9)],
            send_sem=c_send.at[dt],
            recv_sem=c_recv.at[dt],
            device_id={"tm": mate},
            device_id_type=MESH,
        )

    column = lax.broadcasted_iota(jnp.int32, (CHANNELS, LANES), 1)

    def windows(e):
        @pl.loop(0, FORGET)
        def _(n):
            for q in range(4):
                tile = e_buf[n, e, q]
                wide = tile.astype(jnp.float32)
                left = jnp.where(column == 0, 0.0, pltpu.roll(wide, 1, 1)).astype(jnp.bfloat16)
                right = jnp.where(column == LANES - 1, 0.0, pltpu.roll(wide, LANES - 1, 1)).astype(
                    jnp.bfloat16
                )
                for f in range(2):
                    for r in range(2):
                        dt, dh = e - f, q - r
                        if not (0 <= dt < 3 and 0 <= dh < 3):
                            continue
                        lanes = pl.ds(
                            pl.multiple_of(n * 4 * LANES, LANES) + (f * 2 + r) * LANES, LANES
                        )
                        for dw, shifted in enumerate((left, tile, right)):
                            at = (dt * 9 + dh * 3 + dw) * CHANNELS
                            w_buf[at : at + CHANNELS, lanes] = shifted

    def taps_of(dt):
        at = dt * 9 * CHANNELS
        t_buf[dt * 9 : dt * 9 + 9] = jnp.dot(
            w_buf[at : at + 9 * CHANNELS, :], p_buf[...], preferred_element_type=jnp.float32
        ).reshape(9, CHANNELS, OUT)
        pair_copy(dt).start()

    for i in (1, 2):

        @pl.when(receives[i])
        def _():
            halo(i).wait_recv()

    windows(2)
    windows(3)
    taps_of(2)

    def plane_copy(p, d):
        return pltpu.make_async_remote_copy(
            src_ref=s_buf.at[p, d],
            dst_ref=r_buf.at[p, d],
            send_sem=s_send.at[p, d],
            recv_sem=s_recv.at[p, d],
            device_id={"height": lax.rem(me + d, CHIPS)},
            device_id_type=MESH,
        )

    def chunk(p, d):
        chip = lax.rem(me + d, CHIPS)
        low = chip // SUB
        taps = pl.ds(9 * p, 9)
        rows = pl.ds(pl.multiple_of(lax.rem(chip, SUB) * SUB, SUB), SUB)
        own = t_buf[taps, rows, pl.ds(pl.multiple_of((2 * core + low) * LANES, LANES), LANES)]
        other = c_buf[taps, rows, pl.ds(pl.multiple_of(low * LANES, LANES), LANES)]
        return (own + other).reshape(PIECE, LANES)

    def plane_start(p):
        pair_copy(p).wait_recv()

        @pl.loop(1, CHIPS)
        def _(d):
            s_buf[p, d] = chunk(p, d).astype(jnp.bfloat16)
            plane_copy(p, d).start()

        acc[p] = chunk(p, 0)

    def z_copy(p):
        return pltpu.make_async_remote_copy(
            src_ref=z_out.at[p],
            dst_ref=z_in.at[p],
            send_sem=z_send.at[p],
            recv_sem=z_recv.at[p],
            device_id={"tm": far},
            device_id_type=MESH,
        )

    def plane_finish(p):
        @pl.loop(1, CHIPS)
        def _(d):
            plane_copy(p, d).wait_recv()
            acc[p] += r_buf[p, d].astype(jnp.float32)

        z_out[p] = acc[p].astype(jnp.bfloat16)
        z_copy(p).start()

    def place(d):
        owner = lax.rem(me - d + CHIPS, CHIPS)
        return 2 * core + owner // SUB, lax.rem(owner, SUB)

    def gather_copy(p, d):
        kb, cb = place(0)
        return pltpu.make_async_remote_copy(
            src_ref=g_buf.at[p, kb, cb],
            dst_ref=g_buf.at[p, kb, cb],
            send_sem=g_send.at[p, d],
            recv_sem=g_recv.at[p, d],
            device_id={"height": lax.rem(me + d, CHIPS)},
            device_id_type=MESH,
        )

    def hand_copy(p, d):
        kb, cb = place(d)
        return pltpu.make_async_remote_copy(
            src_ref=g_buf.at[p, kb, cb],
            dst_ref=g_buf.at[p, kb, cb],
            send_sem=f_send.at[p, d],
            recv_sem=f_recv.at[p, d],
            device_id={"tm": mate},
            device_id_type=MESH,
        )

    def z_finish(p):
        z_copy(p).wait_recv()
        kb, cb = place(0)
        g_buf[p, kb, cb] = (acc[p] + z_in[p].astype(jnp.float32)).astype(jnp.bfloat16)

        @pl.loop(1, CHIPS)
        def _(d):
            gather_copy(p, d).start()

        hand_copy(p, 0).start()

    def rotate(which, p):
        sides = [
            g_buf[p, 2 * which + i].astype(jnp.float32).reshape(DEPTH, LANES).astype(jnp.bfloat16)
            for i in range(2)
        ]
        rot_buf[which] += jnp.dot(
            b_buf[p], jnp.concatenate(sides, axis=1), preferred_element_type=jnp.float32
        )

    def gather_finish(p):
        @pl.loop(1, CHIPS)
        def _(d):
            gather_copy(p, d).wait_recv()
            hand_copy(p, d).start()

        rotate(core, p)

    def hand_finish(p):
        @pl.loop(0, CHIPS)
        def _(d):
            hand_copy(p, d).wait_recv()

        rotate(1 - core, p)

    def panel_copy(d):
        return pltpu.make_async_remote_copy(
            src_ref=q_buf.at[d],
            dst_ref=y_buf.at[d],
            send_sem=q_send.at[d],
            recv_sem=q_recv.at[d],
            device_id={"panel": lax.rem(panel + d, PANELS)},
            device_id_type=MESH,
        )

    def panel_start(which):
        fin_buf[pl.ds(4 * which, 4)] = rot_buf[which].T.reshape(4, CHANNELS, ROWS)

        @pl.loop(0, 4)
        def _(i):
            target = 4 * which + i

            @pl.when(target != panel)
            def _():
                d = lax.rem(target - panel + PANELS, PANELS)
                q_buf[d] = fin_buf[target].astype(jnp.bfloat16)
                panel_copy(d).start()

    @pl.when(receives[0])
    def _():
        halo(0).wait_recv()

    for i in (3, 4):

        @pl.when(sends[i])
        def _():
            halo(i).start()

    for i in (3, 4):

        @pl.when(receives[i])
        def _():
            halo(i).wait_recv()

    windows(1)
    plane_start(2)
    taps_of(1)
    windows(0)
    plane_start(1)
    taps_of(0)
    plane_finish(2)
    plane_start(0)
    plane_finish(1)

    loads[3].wait()
    loads[4].wait()

    for cb in range(SUB):
        first = cb * ROWS // LANES * LANES
        last = min(first + 3 * LANES, bt_ref.shape[1])
        row = lax.broadcasted_iota(jnp.int32, (ROWS, last - first), 0)
        col = lax.broadcasted_iota(jnp.int32, (ROWS, last - first), 1)
        wanted = cb * ROWS - first + lax.rem(row, SUB) * TAPS + row // SUB
        pick = jnp.where(col == wanted, 1.0, 0.0).astype(jnp.bfloat16)
        moved = lax.dot_general(
            pick,
            bt_ref[:, first:last],
            (((1,), (1,)), ((), ())),
            preferred_element_type=jnp.float32,
        )
        for p in range(PARTS):
            m_buf[p, cb * PIECE : (cb + 1) * PIECE, :] = moved[p * PIECE : (p + 1) * PIECE]
    for p in range(PARTS):
        b_buf[p] = m_buf[p].T.astype(jnp.bfloat16)
    rot_buf[...] = jnp.zeros_like(rot_buf)

    plane_finish(0)
    z_finish(2)
    z_finish(1)
    gather_finish(2)
    hand_finish(2)
    z_finish(0)
    gather_finish(1)
    hand_finish(1)
    gather_finish(0)
    panel_start(core)
    hand_finish(0)
    panel_start(1 - core)

    out_ref[...] = fin_buf[panel]

    @pl.loop(1, PANELS)
    def _(d):
        panel_copy(d).wait_recv()
        out_ref[...] += y_buf[d].astype(jnp.float32)

    out_ref[...] = out_ref[...] / (eig_ref[...] + damping)

    for i in range(5):

        @pl.when(sends[i])
        def _():
            halo(i).wait_send()

    for p in range(PARTS):
        pair_copy(p).wait_send()
        z_copy(p).wait_send()
        hand_copy(p, 0).wait_send()

        @pl.loop(1, CHIPS)
        def _(d):
            plane_copy(p, d).wait_send()
            gather_copy(p, d).wait_send()
            hand_copy(p, d).wait_send()

    @pl.loop(1, PANELS)
    def _(d):
        panel_copy(d).wait_send()


def body(activations, out_grad, out_basis, in_basis, eigenvalues, forget_order):
    dma = pltpu.SemaphoreType.DMA
    bf16, f32 = jnp.bfloat16, jnp.float32
    vmem = pl.BlockSpec(memory_space=pltpu.VMEM)
    positions = BLOCKS * LANES
    return pl.pallas_call(
        kernel,
        out_shape=jax.ShapeDtypeStruct(eigenvalues.shape, f32),
        in_specs=[pl.BlockSpec(memory_space=pltpu.SMEM)] + [pl.BlockSpec(memory_space=pl.ANY)] * 5,
        out_specs=vmem,
        scratch_shapes=[
            pltpu.VMEM(activations.shape, bf16),
            pltpu.VMEM(out_grad.shape, bf16),
            pltpu.VMEM(out_basis.shape, bf16),
            pltpu.VMEM(in_basis.shape[::-1], bf16),
            pltpu.VMEM(eigenvalues.shape, f32),
            dma((5,)),
            pltpu.VMEM((FORGET, 4, 4, CHANNELS, LANES), bf16),
            pltpu.VMEM((TAPS * CHANNELS, positions), bf16),
            pltpu.VMEM((positions, OUT), bf16),
            pltpu.VMEM((TAPS, CHANNELS, OUT), f32),
            pltpu.VMEM((TAPS, CHANNELS, OUT // 2), f32),
            pltpu.VMEM((PARTS, CHIPS, PIECE, LANES), bf16),
            pltpu.VMEM((PARTS, CHIPS, PIECE, LANES), bf16),
            pltpu.VMEM((PARTS, PIECE, LANES), f32),
            pltpu.VMEM((PARTS, PIECE, LANES), bf16),
            pltpu.VMEM((PARTS, PIECE, LANES), bf16),
            pltpu.VMEM((PARTS, 4, SUB, PIECE, LANES), bf16),
            pltpu.VMEM((PARTS, DEPTH, ROWS), f32),
            pltpu.VMEM((PARTS, ROWS, DEPTH), bf16),
            pltpu.VMEM((2, ROWS, 2 * LANES), f32),
            pltpu.VMEM((PANELS, CHANNELS, ROWS), f32),
            pltpu.VMEM((PANELS, CHANNELS, ROWS), bf16),
            pltpu.VMEM((PANELS, CHANNELS, ROWS), bf16),
            dma((5,)),
            dma((5,)),
            dma((3,)),
            dma((3,)),
            dma((PARTS, CHIPS)),
            dma((PARTS, CHIPS)),
            dma((PARTS,)),
            dma((PARTS,)),
            dma((PARTS, CHIPS)),
            dma((PARTS, CHIPS)),
            dma((PARTS, CHIPS)),
            dma((PARTS, CHIPS)),
            dma((PANELS,)),
            dma((PANELS,)),
        ],
        compiler_params=pltpu.CompilerParams(
            collective_id=0, has_side_effects=True, vmem_limit_bytes=56 * 1024 * 1024
        ),
    )(forget_order, activations, out_grad, out_basis, in_basis.T, eigenvalues)


def solution(mesh):
    in_specs = (
        P(None, "tm", "height", "panel", None),
        P(None, "tm", "height", None, None),
        P(),
        P("panel", ("tm", "height")),
        P("panel", ("tm", "height")),
        P(),
    )
    out_specs = P("panel", ("tm", "height"))
    return jax.shard_map(body, mesh=mesh, in_specs=in_specs, out_specs=out_specs, check_vma=False)
```
